32 devices in a mesh: dp: 8 (over z, y), mp: 4 (over x, core).
Axes of the slice: x: 2, y: 2, z: 4, core: 2. Of those that a mesh axis runs over, the one named last changes fastest.
Arguments:
- token_ids: int32 [16384], P('dp'), may hold values from 0 to 8191
- seg_ids: int32 [16384], P('dp'), may hold values from 0 to 255, as said below
- timesteps: int32 [16384], P('dp'), may hold values from 0 to 1999
- noise: float32 [16384, 128], P('dp'), may hold values from -6 to 6
- table: bfloat16 [8192, 128], P('dp'), may hold values from -6 to 6
- w_in: bfloat16 [128, 768], replicated, may hold values from -0.5 to 0.5
- b_in: float32 [768], replicated, may hold values from -3 to 3
- w_time: bfloat16 [128, 768], replicated, may hold values from -0.5 to 0.5
- gain1: float32 [768], replicated, may hold values from 0.5 to 1.5
- shift1: float32 [768], replicated, may hold values from -2 to 2
- w_qkv: bfloat16 [3, 768, 768], P(None, None, 'mp'), may hold values from -0.21875 to 0.21875
- w_out: bfloat16 [768, 768], P('mp'), may hold values from -3.5 to 3.5
- gain2: float32 [768], replicated, may hold values from 0.5 to 1.5
- shift2: float32 [768], replicated, may hold values from -2 to 2
- w_up: bfloat16 [768, 3072], P(None, 'mp'), may hold values from -0.21875 to 0.21875
- b_up: float32 [3072], P('mp'), may hold values from -2 to 2
- w_down: bfloat16 [3072, 768], P('mp'), may hold values from -0.109375 to 0.109375
- b_down: float32 [768], replicated, may hold values from -2 to 2
- cotangent: float32 [16384, 768], P('dp'), may hold values from -6 to 6
Outputs:
- output: float32 [16384, 768], P('dp')
- grad_table: float32 [8192, 128], P('dp')
- grad_w_in: float32 [128, 768], replicated
- grad_b_in: float32 [768], replicated
- grad_w_time: float32 [128, 768], replicated
- grad_gain1: float32 [768], replicated
- grad_shift1: float32 [768], replicated
- grad_w_qkv: float32 [3, 768, 768], P(None, None, 'mp')
- grad_w_out: float32 [768, 768], P('mp')
- grad_gain2: float32 [768], replicated
- grad_shift2: float32 [768], replicated
- grad_w_up: float32 [768, 3072], P(None, 'mp')
- grad_b_up: float32 [3072], P('mp')
- grad_w_down: float32 [3072, 768], P('mp')
- grad_b_down: float32 [768], replicated
The draws below stay inside these ranges and needn't reach their ends.
Inputs may be any that keep to these rules, and one draw needn't show every extreme that they name: `seg_ids`: slots fall into aligned runs of 1024; each run is either one document or 16 documents of 64 slots; ids never fall along the slots and differ between runs; the first run is one document and the last is split.
All inputs are finite; a program needn't handle non-finite values.
Results may differ from the reference program's by a relative error of at most 0.017.
Values may be sent and summed in bfloat16 or wider, within the bound.
No kernel may reach another device: no remote copies, remote signals or barrier semaphores. Data moves between devices by JAX's collectives and lax.ppermute only.
A program may use at most 192 MiB of HBM per device.

```python
import math
import jax
import jax.numpy as jnp
import numpy as np
from jax import lax

D = 768
HEADS = 12
HD = 64
FF = 3072
E = 128
V = 8192
TF = 128
TSTEPS = 2000
SEQ_LONG = 1024
SEQ_SHORT = 64
TOK_DEV = 2048
TOKENS = 16384


def draw_seg_ids(key, part):
    run_total = TOKENS // SEQ_LONG
    per_run = SEQ_LONG // SEQ_SHORT
    kinds = jax.random.randint(jax.random.fold_in(key, 11), (run_total,), 0, 2)
    kinds = kinds.at[0].set(1).at[run_total - 1].set(0)
    places = jnp.arange(TOKENS, dtype=jnp.int32)
    run_of = places // SEQ_LONG
    inside = places % SEQ_LONG // SEQ_SHORT
    long_run = jnp.take(kinds, run_of) == 1
    return (run_of * per_run + jnp.where(long_run, 0, inside)).astype(jnp.int32)


def touch_ends(result, stream_key, smallest, high):
    place = [jax.random.randint(jax.random.fold_in(stream_key, axis), (), 0, length) for axis, length in enumerate(result.shape)]
    widest = result.shape.index(max(result.shape))
    next_to = place[:widest] + [(place[widest] + 1) % result.shape[widest]] + place[widest + 1:]
    return result.at[tuple(place)].set(smallest).at[tuple(next_to)].set(high)


def block_levels(key, dims, cuts, least, top_value):
    def one(axis_at, parts):
        steps = jax.random.uniform(jax.random.fold_in(jax.random.fold_in(key, 6), axis_at), (parts,), jnp.float32, least / len(cuts), top_value / len(cuts))
        return jnp.repeat(jnp.exp(steps), dims[axis_at] // parts).reshape((-1,) + (1,) * (len(dims) - axis_at - 1))

    loudness = one(*cuts[0])
    for cut in cuts[1:]:
        loudness = loudness * one(*cut)
    return loudness


def rank_bounds(number_of, skew):
    weights = [(1 << 20) // math.isqrt(grade ** skew) + 1 for grade in range(1, number_of + 1)]
    scale = 1 + sum(weights) // (1 << 30)
    return np.cumsum(np.array([max(1, weight // scale) for weight in weights]))


def skewed_ids(stream_key, shape, number_of, skew):
    listing = rank_bounds(number_of, skew)
    lot = jax.random.randint(jax.random.fold_in(stream_key, 1), shape, 0, int(listing[number_of - 1]))
    standing = jnp.searchsorted(jnp.asarray(listing, jnp.int32), lot, side="right")
    return jax.random.permutation(jax.random.fold_in(stream_key, 2), number_of)[standing].astype(jnp.int32)


def scatter_about(key, extent, width, limit, shards=(), held_as=jnp.bfloat16):
    drawn = width * jax.random.normal(key, extent, jnp.float32)
    if shards:
        drawn = drawn * block_levels(key, extent, shards, -0.22, 0.18)
    return jnp.clip(drawn, -limit, limit).astype(held_as)


def setup_inputs(seed: int = 0) -> dict:
    keys = jax.random.split(jax.random.key(seed), 20)
    return {
        "token_ids": touch_ends(skewed_ids(keys[0], (TOKENS,), V, 2), jax.random.fold_in(keys[0], 3), 0, V - 1).astype(jnp.int32),
        "seg_ids": draw_seg_ids(jax.random.fold_in(keys[19], 71), 0),
        "timesteps": touch_ends(jax.random.randint(keys[2], (TOKENS,), 0, TSTEPS), jax.random.fold_in(keys[2], 1), 0, TSTEPS - 1).astype(jnp.int32),
        "noise": scatter_about(keys[3], (TOKENS, E), 1.0, 6.0, ((0, 8),), jnp.float32),
        "table": scatter_about(keys[4], (V, E), 1.0, 6.0, ((0, 8),)),
        "w_in": scatter_about(keys[5], (E, D), E ** -0.5, 0.5),
        "b_in": scatter_about(keys[6], (D,), 0.5, 3.0, (), jnp.float32),
        "w_time": scatter_about(keys[7], (TF, D), TF ** -0.5, 0.5),
        "gain1": jnp.clip(1.0 + 0.1 * jax.random.normal(keys[8], (D,), jnp.float32), 0.5, 1.5),
        "shift1": scatter_about(keys[9], (D,), 0.3, 2.0, (), jnp.float32),
        "w_qkv": scatter_about(keys[10], (3, D, HEADS * HD), D ** -0.5, 0.21875, ((2, 4),)),
        "w_out": scatter_about(keys[11], (HEADS * HD, D), (max(D // 256, 1)) ** -0.5, 3.5, ((0, 4),)),
        "gain2": jnp.clip(1.0 + 0.1 * jax.random.normal(keys[12], (D,), jnp.float32), 0.5, 1.5),
        "shift2": scatter_about(keys[13], (D,), 0.3, 2.0, (), jnp.float32),
        "w_up": scatter_about(keys[14], (D, FF), D ** -0.5, 0.21875, ((1, 4),)),
        "b_up": scatter_about(keys[15], (FF,), 0.3, 2.0, ((0, 4),), jnp.float32),
        "w_down": scatter_about(keys[16], (FF, D), FF ** -0.5, 0.109375, ((0, 4),)),
        "b_down": scatter_about(keys[17], (D,), 0.3, 2.0, (), jnp.float32),
        "cotangent": scatter_about(keys[18], (TOKENS, D), 1.0, 6.0, ((0, 8),), jnp.float32),
    }


@jax.custom_vjp
def low(v):
    return lax.optimization_barrier(v.astype(jnp.bfloat16)).astype(jnp.float32)

@jax.custom_vjp
def low_back(v):
    return v

def low_keep(v):
    return (low(v), None)

def low_pass(kept, grad):
    return (grad,)

def back_keep(v):
    return (v, None)

def back_low(kept, grad):
    return (low(grad),)
low.defvjp(low_keep, low_pass)
low_back.defvjp(back_keep, back_low)
NEG_BIG = -1000000000.0

def matmul_high(left, right):
    return jnp.dot(left, right, precision=lax.Precision.HIGHEST, preferred_element_type=jnp.float32)

def layer_norm(inputs, gain_vec, shift_vec):
    row_mean = lax.optimization_barrier(jnp.mean(inputs, axis=-1, keepdims=True))
    centred = inputs - row_mean
    variance = lax.optimization_barrier(jnp.mean(centred * centred, axis=-1, keepdims=True))
    return centred * lax.rsqrt(variance + 1e-05) * gain_vec + shift_vec

def noise_rates(time_ids, horizon):
    fraction = time_ids.astype(jnp.float32) / horizon
    signal = 1.0 - jnp.sqrt(fraction + 0.0001)
    return (jnp.sqrt(signal), jnp.sqrt(1.0 - signal))

def time_features(time_ids, feat_width):
    half_width = feat_width // 2
    freq_table = jnp.exp(-math.log(10000.0) * jnp.arange(half_width, dtype=jnp.float32) / half_width)
    angles = time_ids.astype(jnp.float32)[:, None] * freq_table[None, :]
    return jnp.concatenate([jnp.sin(angles), jnp.cos(angles)], axis=1)

def attention_row(pieces):
    queries, keys_row, values_row, seg_row = pieces
    scaled = low_back(jnp.einsum('qhd,khd->hqk', queries, keys_row, precision=lax.Precision.HIGHEST) * HD ** (-0.5))
    same_seg = seg_row[:, None] == seg_row[None, :]
    scores = jnp.where(same_seg[None], scaled, NEG_BIG)
    row_top = lax.optimization_barrier(jnp.max(scores, axis=-1, keepdims=True))
    exponent = jnp.exp(scores - row_top)
    attn_probs = low(exponent / lax.optimization_barrier(jnp.sum(exponent, axis=-1, keepdims=True)))
    return jnp.einsum('hqk,khd->qhd', attn_probs, values_row, precision=lax.Precision.HIGHEST)

def reference(token_ids, seg_ids, timesteps, noise, table, w_in, b_in, w_time, gain1, shift1, w_qkv, w_out, gain2, shift2, w_up, b_up, w_down, b_down, cotangent):
    keep_rate, noise_rate = noise_rates(timesteps, TSTEPS)
    features = low(time_features(timesteps, TF))
    row_count = TOKENS // TOK_DEV
    seg_rows = seg_ids.reshape(row_count, TOK_DEV)
    row_attention = jax.checkpoint(attention_row)

    def forward(param_table, param_w_in, param_b_in, param_w_time, param_gain1, param_shift1, param_w_qkv, param_w_out, param_gain2, param_shift2, param_w_up, param_b_up, param_w_down, param_b_down):
        row_norms = jnp.sqrt(lax.optimization_barrier(jnp.sum(param_table * param_table, axis=1)) + 1e-06)
        factor = math.sqrt(E) / jnp.mean(row_norms)
        clean_rows = jnp.take(param_table, token_ids, axis=0) * factor
        noisy_in = low(keep_rate[:, None] * clean_rows + noise_rate[:, None] * noise)
        hidden = low_back(matmul_high(noisy_in, param_w_in) + matmul_high(features, param_w_time) + param_b_in)
        act_one = low(layer_norm(hidden, param_gain1, param_shift1))
        projected = low(low_back(jnp.einsum('td,cdk->ctk', act_one, param_w_qkv, precision=lax.Precision.HIGHEST)))
        heads_all = projected.reshape(3, row_count, TOK_DEV, HEADS, HD)
        mixed_rows = lax.map(row_attention, (heads_all[0], heads_all[1], heads_all[2], seg_rows))
        mixed = low(low_back(mixed_rows)).reshape(TOKENS, HEADS * HD)
        attn_out = low_back(matmul_high(mixed, param_w_out))
        resid = hidden + attn_out
        act_two = low(layer_norm(resid, param_gain2, param_shift2))
        pre_act = low_back(matmul_high(act_two, param_w_up) + param_b_up)
        activated = low(jax.nn.gelu(pre_act, approximate=False))
        return resid + low_back(matmul_high(activated, param_w_down)) + param_b_down
    params = (table.astype(jnp.float32), w_in.astype(jnp.float32), b_in.astype(jnp.float32), w_time.astype(jnp.float32), gain1.astype(jnp.float32), shift1.astype(jnp.float32), w_qkv.astype(jnp.float32), w_out.astype(jnp.float32), gain2.astype(jnp.float32), shift2.astype(jnp.float32), w_up.astype(jnp.float32), b_up.astype(jnp.float32), w_down.astype(jnp.float32), b_down.astype(jnp.float32))
    output, backward = jax.vjp(forward, *params)
    grads = backward(cotangent)
    return (output, grads[0], grads[1], grads[2], grads[3], grads[4], grads[5], grads[6], grads[7], grads[8], grads[9], grads[10], grads[11], grads[12], grads[13])
```

```python
import math

import jax
import jax.numpy as jnp
from jax import lax
from jax.experimental import pallas as pl
from jax.experimental.pallas import tpu as pltpu
from jax.sharding import PartitionSpec as P

HD = 64
TSTEPS = 2000
SEQ_LONG = 1024
SEQ_SHORT = 64
EPS = 1e-05
NEG_BIG = -1000000000.0
BF = jnp.bfloat16
F32 = jnp.float32
CORE, XDIR = 1, 2


def swap(array_in, axis, bit_mask):
    pairs = [(i, i ^ bit_mask) for i in range(lax.axis_size(axis))]
    return lax.ppermute(array_in, axis, pairs)


def mm(left, right):
    return jnp.dot(left, right, preferred_element_type=F32)


def mm_t(left, right):
    return lax.dot_general(left, right, (((1,), (1,)), ((), ())), preferred_element_type=F32)


def t_mm(left, right):
    return lax.dot_general(left, right, (((0,), (0,)), ((), ())), preferred_element_type=F32)


def call(kernel, grid, in_specs, out_specs, out_shape, scratch=(), flops=0, moved=0, name=None):
    return pl.pallas_call(
        kernel,
        grid_spec=pltpu.PrefetchScalarGridSpec(
            num_scalar_prefetch=1,
            grid=grid,
            in_specs=in_specs,
            out_specs=out_specs,
            scratch_shapes=list(scratch),
        ),
        out_shape=out_shape,
        compiler_params=pltpu.CompilerParams(dimension_semantics=("arbitrary",) * len(grid)),
        cost_estimate=pl.CostEstimate(flops=flops, bytes_accessed=moved, transcendentals=0),
        name=name,
    )


def sds(shape, dtype):
    return jax.ShapeDtypeStruct(shape, dtype)


def rows(block, width):
    return pl.BlockSpec((block, width), lambda i, s: (i, 0))


def whole(shape):
    return pl.BlockSpec(shape, lambda *a: (0,) * len(shape))


def lookup_kernel(scal, ids_ref, table_ref, out_ref, acc):
    step = pl.program_id(0)
    width = table_ref.shape[0]
    lanes = lax.broadcasted_iota(jnp.int32, (ids_ref.shape[0], width), 1) + step * width
    hot = (ids_ref[...] == lanes).astype(F32).astype(BF)
    part = mm(hot, table_ref[...])

    @pl.when(step == 0)
    def _():
        acc[...] = part

    @pl.when(step > 0)
    def _():
        acc[...] += part

    @pl.when(step == pl.num_programs(0) - 1)
    def _():
        out_ref[...] = acc[...].astype(BF)


def lookup(scal, ids_col, table_rows):
    tokens, width = ids_col.shape[0], table_rows.shape[1]
    blk = 512
    return call(
        lookup_kernel,
        (table_rows.shape[0] // blk,),
        [whole((tokens, 1)), rows(blk, width)],
        whole((tokens, width)),
        sds((tokens, width), BF),
        [pltpu.VMEM((tokens, width), F32)],
        flops=2 * tokens * table_rows.size,
        moved=2 * table_rows.size,
        name="lookup",
    )(scal, ids_col, table_rows)


def scatter_kernel(scal, ids_ref, grad_ref, out_ref):
    blk = out_ref.shape[0]
    row_no = lax.broadcasted_iota(jnp.int32, (blk, ids_ref.shape[1]), 0) + pl.program_id(0) * blk
    hot = (ids_ref[...] == row_no).astype(F32).astype(BF)
    out_ref[...] = mm(hot, grad_ref[...]).astype(BF)


def scatter(scal, ids_row, grad_rows, row_count):
    tokens, width = grad_rows.shape
    blk = 512
    return call(
        scatter_kernel,
        (row_count // blk,),
        [whole((1, tokens)), whole((tokens, width))],
        rows(blk, width),
        sds((row_count, width), BF),
        flops=2 * tokens * row_count * width,
        moved=2 * row_count * width,
        name="scatter",
    )(scal, ids_row, grad_rows)


def project_kernel(scal, noisy, feat, w_in, w_time, b_in, gain, shift, w_qkv, hid, act, q, k, v):
    hidden = mm(noisy[...], w_in[...]) + mm(feat[...], w_time[...]) + b_in[...]
    hid[...] = hidden
    mean = jnp.mean(hidden, axis=-1, keepdims=True)
    centred = hidden - mean
    var = jnp.mean(centred * centred, axis=-1, keepdims=True)
    normed = (centred * lax.rsqrt(var + EPS) * gain[...] + shift[...]).astype(BF)
    act[...] = normed
    kw = q.shape[1]
    q[...] = (mm_t(normed, w_qkv[0:kw, :]).astype(BF) * HD**-0.5).astype(BF)
    k[...] = mm_t(normed, w_qkv[kw : 2 * kw, :]).astype(BF)
    v[...] = mm_t(normed, w_qkv[2 * kw : 3 * kw, :]).astype(BF)


def project(scal, noisy, feat, w_in, w_time, b_in, gain, shift, w_qkv):
    tokens, embed = noisy.shape
    wide = w_in.shape[1]
    kw = w_qkv.shape[0] // 3
    blk = 256
    return call(
        project_kernel,
        (tokens // blk,),
        [
            rows(blk, embed),
            rows(blk, feat.shape[1]),
            whole(w_in.shape),
            whole(w_time.shape),
            whole((1, wide)),
            whole((1, wide)),
            whole((1, wide)),
            whole(w_qkv.shape),
        ],
        [rows(blk, wide), rows(blk, wide), rows(blk, kw), rows(blk, kw), rows(blk, kw)],
        [sds((tokens, wide), F32), sds((tokens, wide), BF)] + [sds((tokens, kw), BF)] * 3,
        flops=2 * tokens * wide * (2 * embed + 3 * kw),
        moved=tokens * wide * 9,
        name="project",
    )(scal, noisy, feat, w_in, w_time, b_in, gain, shift, w_qkv)


def own_lanes(array_in, head):
    lane = lax.broadcasted_iota(jnp.int32, array_in.shape, 1)
    return jnp.where((lane < HD) == (head == 0), array_in, jnp.zeros_like(array_in))


def short_mask(scores):
    key_doc = lax.broadcasted_iota(jnp.int32, scores.shape, 0) // SEQ_SHORT
    query_doc = lax.broadcasted_iota(jnp.int32, scores.shape, 1) // SEQ_SHORT
    return key_doc == query_doc


def attend_kernel(scal, q_ref, k_ref, v_ref, mixed_ref, lse_ref, v_t):
    step = pl.program_id(1)
    blk = q_ref.shape[0]

    @pl.when(step == 0)
    def _():
        v_t[...] = v_ref[...].T

    def run(key_rows, value_cols, masked):
        parts = []
        for head in range(2):
            scores = mm_t(key_rows, own_lanes(q_ref[...], head))
            if masked:
                scores = jnp.where(short_mask(scores), scores, NEG_BIG)
            top = jnp.max(scores, axis=0, keepdims=True)
            weights = jnp.exp(scores - top)
            total = jnp.sum(weights, axis=0, keepdims=True)
            part = mm(value_cols[head * HD : (head + 1) * HD, :], weights.astype(BF))
            parts.append(part * (1.0 / total))
            lse_ref[0, head : head + 1, :] = top + jnp.log(total)
        mixed_ref[...] = jnp.concatenate(parts, axis=0).T.astype(BF)

    @pl.when(scal[2] == 1)
    def _():
        run(k_ref[...], v_t[...], False)

    @pl.when(scal[2] == 0)
    def _():
        start = pl.multiple_of(step * blk, blk)
        run(k_ref[pl.ds(start, blk), :], v_t[:, pl.ds(start, blk)], True)


def attend(scal, q, k, v):
    tokens, kw = q.shape
    pair = 2 * HD
    blk = 256
    qspec = pl.BlockSpec((blk, pair), lambda p, i, s: (i, p))
    kspec = pl.BlockSpec((tokens, pair), lambda p, i, s: (0, p))
    return call(
        attend_kernel,
        (kw // pair, tokens // blk),
        [qspec, kspec, kspec],
        [qspec, pl.BlockSpec((1, 8, blk), lambda p, i, s: (p, 0, i))],
        [sds((tokens, kw), BF), sds((kw // pair, 8, tokens), F32)],
        [pltpu.VMEM((pair, tokens), BF)],
        flops=16 * tokens * tokens * kw,
        moved=8 * tokens * kw,
        name="attend",
    )(scal, q, k, v)


def attend_back_kernel(scal, q_ref, k_ref, v_ref, g_ref, lse_ref, dq_ref, dk_ref, dv_ref, k_t, dk, dv):
    step = pl.program_id(1)
    blk = q_ref.shape[0]

    @pl.when(step == 0)
    def _():
        k_t[...] = k_ref[...].T
        dk[...] = jnp.zeros_like(dk)
        dv[...] = jnp.zeros_like(dv)

    def run(where, masked):
        key_rows, value_rows, key_cols = k_ref[where, :], v_ref[where, :], k_t[:, where]
        parts = []
        for head in range(2):
            query = own_lanes(q_ref[...], head)
            grad = own_lanes(g_ref[...], head)
            scores = mm_t(key_rows, query)
            if masked:
                scores = jnp.where(short_mask(scores), scores, NEG_BIG)
            probs = jnp.exp(scores - lse_ref[0, head : head + 1, :])
            grad_probs = mm_t(value_rows, grad)
            both = probs * grad_probs
            delta = jnp.sum(both, axis=0, keepdims=True)
            grad_scores = (both - probs * delta).astype(BF)
            dv[where, :] += mm(probs.astype(BF), grad)
            dk[where, :] += mm(grad_scores, query)
            parts.append(mm(key_cols[head * HD : (head + 1) * HD, :], grad_scores))
        dq_ref[...] = (jnp.concatenate(parts, axis=0).T * HD**-0.5).astype(BF)

    @pl.when(scal[2] == 1)
    def _():
        run(slice(None), False)

    @pl.when(scal[2] == 0)
    def _():
        run(pl.ds(pl.multiple_of(step * blk, blk), blk), True)

    @pl.when(step == pl.num_programs(1) - 1)
    def _():
        dk_ref[...] = dk[...].astype(BF)
        dv_ref[...] = dv[...].astype(BF)


def attend_back(scal, q, k, v, grad, lse):
    tokens, kw = q.shape
    pair = 2 * HD
    blk = 256
    qspec = pl.BlockSpec((blk, pair), lambda p, i, s: (i, p))
    kspec = pl.BlockSpec((tokens, pair), lambda p, i, s: (0, p))
    return call(
        attend_back_kernel,
        (kw // pair, tokens // blk),
        [qspec, kspec, kspec, qspec, pl.BlockSpec((1, 8, blk), lambda p, i, s: (p, 0, i))],
        [qspec, kspec, kspec],
        [sds((tokens, kw), BF)] * 3,
        [pltpu.VMEM((pair, tokens), BF), pltpu.VMEM((tokens, pair), F32), pltpu.VMEM((tokens, pair), F32)],
        flops=40 * tokens * tokens * kw,
        moved=14 * tokens * kw,
        name="attend_back",
    )(scal, q, k, v, grad, lse)


def gelu_pair(pre):
    mag = jnp.abs(pre)
    bell = jnp.exp(-0.5 * pre * pre)
    t = 1.0 / (1.0 + (0.3275911 * 0.5**0.5) * mag)
    poly = t * (0.127414796 + t * (-0.142248368 + t * (0.7107068705 + t * (-0.7265760135 + t * 0.5307027145))))
    tail = poly * bell
    cdf = jnp.where(pre >= 0, 1.0 - tail, tail)
    return cdf, cdf + pre * (bell * (2.0 * math.pi) ** -0.5)


def ffn_kernel(
    scal, hid, own, got, cot, gain, shift, up0, up1, bup0, bup1, dn0, dn1,
    resid, act2, cotr, ac0, ac1, gp0, gp1, down, ga2, gbup,
):
    res = hid[...] + (own[...].astype(F32) + got[...].astype(F32))
    resid[...] = res
    mean = jnp.mean(res, axis=-1, keepdims=True)
    centred = res - mean
    var = jnp.mean(centred * centred, axis=-1, keepdims=True)
    normed = (centred * lax.rsqrt(var + EPS) * gain[...] + shift[...]).astype(BF)
    act2[...] = normed
    cot_low = cot[...].astype(BF)
    cotr[...] = cot_low

    @pl.when(pl.program_id(0) == 0)
    def _():
        gbup[...] = jnp.zeros_like(gbup)

    down_sum, back_sum = None, None
    for half, (up, bup, dn, ac, gp) in enumerate(((up0, bup0, dn0, ac0, gp0), (up1, bup1, dn1, ac1, gp1))):
        pre = mm(normed, up[...]) + bup[...]
        cdf, slope = gelu_pair(pre)
        activated = (pre * cdf).astype(BF)
        ac[...] = activated
        grad_pre = (mm_t(cot_low, dn[...]) * slope).astype(BF)
        gp[...] = grad_pre
        gbup[half : half + 1, :] += jnp.sum(grad_pre.astype(F32), axis=0, keepdims=True)
        d = mm(activated, dn[...])
        b = mm_t(grad_pre, up[...])
        down_sum = d if half == 0 else down_sum + d
        back_sum = b if half == 0 else back_sum + b
    down[...] = down_sum.astype(BF)
    ga2[...] = back_sum.astype(BF)


def ffn(scal, hid, own, got, cot, gain, shift, up0, up1, bup0, bup1, dn0, dn1):
    tokens, wide = hid.shape
    ff = up0.shape[1]
    blk = 256
    steps = tokens // blk
    cot_spec = pl.BlockSpec((blk, wide), lambda i, s: (s[0] * steps + i, 0))
    r = rows(blk, wide)
    f = rows(blk, ff)
    return call(
        ffn_kernel,
        (steps,),
        [r, r, r, cot_spec, whole((1, wide)), whole((1, wide)), whole((wide, ff)), whole((wide, ff)),
         whole((1, ff)), whole((1, ff)), whole((ff, wide)), whole((ff, wide))],
        [r, r, r, f, f, f, f, r, r, whole((8, ff))],
        [sds((tokens, wide), F32), sds((tokens, wide), BF), sds((tokens, wide), BF)]
        + [sds((tokens, ff), BF)] * 4 + [sds((tokens, wide), BF)] * 2 + [sds((8, ff), F32)],
        flops=16 * tokens * wide * ff,
        moved=tokens * wide * 30,
        name="ffn",
    )(scal, hid, own, got, cot, gain, shift, up0, up1, bup0, bup1, dn0, dn1)


def norm_back(base, grad, gain):
    mean = jnp.mean(base, axis=-1, keepdims=True)
    centred = base - mean
    var = jnp.mean(centred * centred, axis=-1, keepdims=True)
    inv = lax.rsqrt(var + EPS)
    normed = centred * inv
    dn = grad * gain
    out = (dn - jnp.mean(dn, axis=-1, keepdims=True) - normed * jnp.mean(dn * normed, axis=-1, keepdims=True)) * inv
    return out, normed


def add_row(ref, row, value):
    ref[row : row + 1, : value.shape[1]] += jnp.sum(value, axis=0, keepdims=True)


def resid_back_kernel(scal, resid, own, got, cot, gain, w_out, grad_res, grad_attn, grad_mixed, vec):
    @pl.when(pl.program_id(0) == 0)
    def _():
        vec[...] = jnp.zeros_like(vec)

    grad = own[...].astype(F32) + got[...].astype(F32)
    back, normed = norm_back(resid[...], grad, gain[...])
    cotangent = cot[...]
    out = cotangent + back
    grad_res[...] = out
    low = out.astype(BF)
    grad_attn[...] = low
    grad_mixed[...] = mm_t(low, w_out[...]).astype(BF)
    add_row(vec, 0, grad * normed)
    add_row(vec, 1, grad)
    add_row(vec, 2, cotangent)


def resid_back(scal, resid, own, got, cot, gain, w_out):
    tokens, wide = resid.shape
    kw = w_out.shape[0]
    blk = 256
    steps = tokens // blk
    r = rows(blk, wide)
    return call(
        resid_back_kernel,
        (steps,),
        [r, r, r, pl.BlockSpec((blk, wide), lambda i, s: (s[0] * steps + i, 0)), whole((1, wide)), whole(w_out.shape)],
        [r, r, rows(blk, kw), whole((8, wide))],
        [sds((tokens, wide), F32), sds((tokens, wide), BF), sds((tokens, kw), BF), sds((8, wide), F32)],
        flops=2 * tokens * wide * kw,
        moved=tokens * wide * 18,
        name="resid_back",
    )(scal, resid, own, got, cot, gain, w_out)


def hidden_back_kernel(scal, hid, own, got, grad_res, gain, w_in, keepf, looked, grad_hid, rows_out, vec):
    @pl.when(pl.program_id(0) == 0)
    def _():
        vec[...] = jnp.zeros_like(vec)

    grad = own[...].astype(F32) + got[...].astype(F32)
    back, normed = norm_back(hid[...], grad, gain[...])
    low = (grad_res[...] + back).astype(BF)
    grad_hid[...] = low
    scaled = mm_t(low, w_in[...]) * keepf[...]
    rows_out[...] = scaled.astype(BF)
    add_row(vec, 0, grad * normed)
    add_row(vec, 1, grad)
    add_row(vec, 2, low.astype(F32))
    add_row(vec, 3, scaled * looked[...].astype(F32))


def hidden_back(scal, hid, own, got, grad_res, gain, w_in, keepf, looked):
    tokens, wide = hid.shape
    embed = w_in.shape[0]
    blk = 256
    r = rows(blk, wide)
    e = rows(blk, embed)
    return call(
        hidden_back_kernel,
        (tokens // blk,),
        [r, r, r, r, whole((1, wide)), whole(w_in.shape), rows(blk, 1), e],
        [r, e, whole((8, wide))],
        [sds((tokens, wide), BF), sds((tokens, embed), BF), sds((8, wide), F32)],
        flops=2 * tokens * wide * embed,
        moved=tokens * wide * 14,
        name="hidden_back",
    )(scal, hid, own, got, grad_res, gain, w_in, keepf, looked)


def bit_of(number, bit):
    return (number >> bit) & 1


def add_low(left, right):
    return (left.astype(F32) + right.astype(F32)).astype(BF)


def sum_over_dp(current, dp, order):
    for bit in order:
        half = current.shape[0] // 2
        mine = bit_of(dp, bit)
        sent = lax.dynamic_slice_in_dim(current, (1 - mine) * half, half, 0)
        kept = lax.dynamic_slice_in_dim(current, mine * half, half, 0)
        current = add_low(kept, swap(sent, "dp", 1 << bit))
    for bit in reversed(order):
        got = swap(current, "dp", 1 << bit)
        mine = bit_of(dp, bit) == 1
        current = jnp.concatenate([jnp.where(mine, got, current), jnp.where(mine, current, got)], axis=0)
    return current


def body(
    token_ids, seg_ids, timesteps, noise, table, w_in, b_in, w_time, gain1, shift1, w_qkv, w_out,
    gain2, shift2, w_up, b_up, w_down, b_down, cotangent,
):
    dp = lax.axis_index("dp")
    dp_count = lax.axis_size("dp")
    dp_bits = dp_count.bit_length() - 1
    mp = lax.axis_index("mp")
    core, xpos = mp % 2, mp // 2
    tokens = token_ids.shape[0] // 2
    table_rows, embed = table.shape
    vocab = table_rows * dp_count
    part_rows = table_rows // 2
    wide = w_in.shape[1]
    kw = w_qkv.shape[2]

    def mine(array_in):
        return lax.dynamic_slice_in_dim(array_in, xpos * tokens, tokens, 0)

    ids, seg, times = mine(token_ids), mine(seg_ids), mine(timesteps)
    scal = jnp.stack([xpos, core, (seg[0] == seg[tokens - 1]).astype(jnp.int32), dp]).astype(jnp.int32)

    qkv_t = jnp.transpose(w_qkv, (0, 2, 1))
    qkv_other = swap(qkv_t.reshape(3 * kw, wide), "mp", XDIR).reshape(3, kw, wide)
    qkv6 = jnp.concatenate([qkv_t, qkv_other], axis=1).reshape(6 * kw, wide)
    out6 = jnp.concatenate([w_out, swap(w_out, "mp", XDIR)], axis=0)
    down_other = swap(w_down, "mp", XDIR)
    up_other = swap(w_up, "mp", XDIR)
    bup_other = swap(b_up.reshape(1, -1), "mp", XDIR)

    held = lax.dynamic_slice_in_dim(table, core * part_rows, part_rows, 0)
    place = [0]
    for bit in reversed(range(dp_bits)):
        held = jnp.concatenate([held, swap(held, "dp", 1 << bit)], axis=0)
        place = place + [at | (1 << bit) for at in place]
    relative = (ids // table_rows) ^ dp
    position = sum(bit_of(relative, bit) << (dp_bits - 1 - bit) for bit in range(dp_bits))
    inside = ids % table_rows
    local = jnp.where(inside // part_rows == core, position * part_rows + inside % part_rows, -1)

    table_f = table.astype(F32)
    row_norms = jnp.sqrt(jnp.sum(table_f * table_f, axis=1, keepdims=True) + 1e-06)
    norm_sum = jnp.full((8, 128), jnp.sum(row_norms), F32)
    for bit in range(dp_bits):
        norm_sum = norm_sum + swap(norm_sum, "dp", 1 << bit)
    mean_norm = norm_sum[0, 0] / vocab
    factor = math.sqrt(embed) / mean_norm

    fraction = times.astype(F32) / TSTEPS
    signal = 1.0 - jnp.sqrt(fraction + 0.0001)
    keepf = (jnp.sqrt(signal) * factor)[:, None]
    spread = jnp.sqrt(1.0 - signal)[:, None]
    half_width = w_time.shape[0] // 2
    freq = jnp.exp(-math.log(10000.0) * jnp.arange(half_width, dtype=F32) / half_width)
    angles = times.astype(F32)[:, None] * freq[None, :]
    features = jnp.concatenate([jnp.sin(angles), jnp.cos(angles)], axis=1).astype(BF)
    looked = lookup(scal, local[:, None], held)
    looked = looked + swap(looked, "mp", CORE)
    noisy = (keepf * looked.astype(F32) + spread * mine(noise)).astype(BF)

    row = lambda vector: vector.reshape(1, -1)
    hidden, act_one, q, k, v = project(
        scal, noisy, features, w_in, w_time, row(b_in), row(gain1), row(shift1), qkv6
    )
    mixed, lse = attend(scal, q, k, v)
    attn_part = mm(mixed, out6).astype(BF)
    attn_got = swap(attn_part, "mp", CORE)

    resid, act_two, cot_low, ac0, ac1, gp0, gp1, down_part, ga2_part, gbup = ffn(
        scal, hidden, attn_part, attn_got, cotangent, row(gain2), row(shift2), w_up, up_other,
        row(b_up), bup_other, w_down, down_other,
    )
    ga2_got = swap(ga2_part, "mp", CORE)
    low_order = list(range(dp_bits))
    high_order = low_order[1:] + low_order[:1]

    def weight_sum(own, other, order):
        total = add_low(own, swap(other, "mp", XDIR))
        return sum_over_dp(total, dp, order)

    grad_w_down = weight_sum(t_mm(ac0, cot_low).astype(BF), t_mm(ac1, cot_low).astype(BF), low_order).astype(F32)
    grad_w_up = weight_sum(t_mm(act_two, gp0).astype(BF), t_mm(act_two, gp1).astype(BF), high_order).astype(F32)
    bias_sum = gbup[0:1] + swap(gbup[1:2], "mp", XDIR)
    for bit in low_order:
        bias_sum = bias_sum + swap(bias_sum, "dp", 1 << bit)

    grad_res, grad_attn, grad_mixed, vec2 = resid_back(scal, resid, ga2_part, ga2_got, cotangent, row(gain2), out6)

    down_got = swap(down_part, "mp", CORE)
    out_own = (resid + (down_part.astype(F32) + down_got.astype(F32)) + b_down).astype(BF)
    out_x = swap(lax.dynamic_slice_in_dim(out_own, core * (tokens // 2), tokens // 2, 0), "mp", XDIR)
    out_c = swap(out_x, "mp", CORE)
    first = core == 0
    out_other = jnp.concatenate([jnp.where(first, out_x, out_c), jnp.where(first, out_c, out_x)], axis=0)
    low_x = xpos == 0
    output = jnp.concatenate(
        [jnp.where(low_x, out_own, out_other), jnp.where(low_x, out_other, out_own)], axis=0
    ).astype(F32)

    dq, dk, dv = attend_back(scal, q, k, v, grad_mixed, lse)
    ga1_part = (
        mm(dq, qkv6[: 2 * kw]) + mm(dk, qkv6[2 * kw : 4 * kw]) + mm(dv, qkv6[4 * kw :])
    ).astype(BF)
    ga1_got = swap(ga1_part, "mp", CORE)
    wide_grads = [t_mm(grad, act_one).astype(BF) for grad in (dq, dk, dv)] + [t_mm(mixed, grad_attn).astype(BF)]
    attn_sum = weight_sum(
        jnp.concatenate([g[:kw] for g in wide_grads], axis=0),
        jnp.concatenate([g[kw:] for g in wide_grads], axis=0),
        low_order,
    )
    grad_w_qkv = jnp.transpose(attn_sum[: 3 * kw].reshape(3, kw, wide), (0, 2, 1)).astype(F32)
    grad_w_out = attn_sum[3 * kw :].astype(F32)

    grad_hid, grad_rows, vec1 = hidden_back(
        scal, hidden, ga1_part, ga1_got, grad_res, row(gain1), w_in, keepf, looked
    )

    direct = scatter(scal, local[None, :], grad_rows, dp_count * part_rows)
    for bit in range(dp_bits):
        half = direct.shape[0] // 2
        direct = add_low(direct[:half], swap(direct[half:], "dp", 1 << bit))
    direct = add_low(direct, swap(direct, "mp", XDIR))
    direct_got = swap(direct, "mp", CORE)

    source = jnp.where(first, noisy, features)
    pack = jnp.concatenate([t_mm(source, grad_hid), vec1[:4], vec2[:4]], axis=0).astype(BF)
    pack = add_low(pack, swap(pack, "mp", XDIR))
    for bit in low_order:
        pack = add_low(pack, swap(pack, "dp", 1 << bit))
    pack_got = swap(pack[:embed], "mp", CORE)
    grad_w_in = jnp.where(first, pack[:embed], pack_got).astype(F32)
    grad_w_time = jnp.where(first, pack_got, pack[:embed]).astype(F32)
    vec = pack[embed:].astype(F32)

    coeff = -jnp.sum(vec[3, :embed]) / (mean_norm * vocab)
    both = jnp.concatenate([jnp.where(first, direct, direct_got), jnp.where(first, direct_got, direct)], axis=0)
    grad_table = both.astype(F32) + coeff * (table_f / row_norms)
    return (
        output, grad_table, grad_w_in, vec[2], grad_w_time, vec[0], vec[1], grad_w_qkv, grad_w_out,
        vec[4], vec[5], grad_w_up, bias_sum[0], grad_w_down, vec[6],
    )


def solution(mesh):
    rep, dp, dp2 = P(), P("dp"), P("dp", None)
    in_specs = (
        dp, dp, dp, dp2, dp2, rep, rep, rep, rep, rep, P(None, None, "mp"), P("mp", None), rep, rep,
        P(None, "mp"), P("mp"), P("mp", None), rep, dp2,
    )
    out_specs = (
        dp2, dp2, rep, rep, rep, rep, rep, P(None, None, "mp"), P("mp", None), rep, rep,
        P(None, "mp"), P("mp"), P("mp", None), rep,
    )
    return jax.shard_map(body, mesh=mesh, in_specs=in_specs, out_specs=out_specs, check_vma=False)
```
